128 devices in a mesh: op: 16 (over z_lo, y, core), sec: 8 (over z_hi, x).
Axes of the slice: x: 4, y: 4, z: 4 (z_hi: 2, z_lo: 2; z = z_hi * 2 + z_lo), core: 2. Of those that a mesh axis runs over, the one named last changes fastest.
Arguments:
- wavefunction: bfloat16 [3, 8, 512, 512], P(None, 'sec'), may hold values from -6 to 6
- left_ops: bfloat16 [256, 512, 512], P('op'), may hold values from -0.015625 to 0.015625
- right_ops: bfloat16 [256, 512, 512], P('op'), may hold values from -0.25 to 0.25
- targets: int32 [256, 8], P('op'), may hold values from 0 to 7, each once within a row
Outputs:
- sigma: bfloat16 [3, 8, 512, 512], P(None, 'sec', 'op')
The draws below stay inside these ranges and needn't reach their ends.
Inputs may be any that keep to these rules, and one draw needn't show every extreme that they name: Each row of targets names every sector exactly once.
All inputs are finite; a program needn't handle non-finite values.
Results may differ from the reference program's by a relative error of at most 0.005.
Values may be sent and summed in bfloat16 or wider, within the bound.
A program may use at most 192 MiB of HBM per device.

```python
import jax
import jax.numpy as jnp
from jax import lax

SB = 512
NVEC = 3
NOP = 256
NSEC = 8


def block_scale(key, dims, shards, low, high):
    def one(position, shards_of):
        heights = jax.random.uniform(jax.random.fold_in(jax.random.fold_in(key, 6), position), (shards_of,), jnp.float32, low / len(shards), high / len(shards))
        return jnp.repeat(jnp.exp(heights), dims[position] // shards_of).reshape((-1,) + (1,) * (len(dims) - position - 1))

    level = one(*shards[0])
    for cut in shards[1:]:
        level = level * one(*cut)
    return level


def gaussian(stream_key, shape, width, reach, pieces=(), held_as=jnp.bfloat16):
    drawn = width * jax.random.normal(stream_key, shape, jnp.float32)
    if pieces:
        drawn = drawn * block_scale(stream_key, shape, pieces, -0.22, 0.18)
    return jnp.clip(drawn, -reach, reach).astype(held_as)


def setup_inputs(seed: int = 0) -> dict:
    arg_keys = jax.random.split(jax.random.key(seed), 5)
    wavefunction = gaussian(arg_keys[0], (NVEC, NSEC, SB, SB), 1.0, 6.0, ((1, 8),))
    left_ops = gaussian(arg_keys[1], (NOP, SB, SB), (SB * NOP) ** -0.5, 0.015625, ((0, 16),))
    right_ops = gaussian(arg_keys[2], (NOP, SB, SB), SB ** -0.5, 0.25, ((0, 16),))
    targets = jax.vmap(lambda own: jax.random.permutation(own, NSEC))(jax.random.split(arg_keys[3], NOP)).reshape((NOP, NSEC)).astype(jnp.int32)
    return {"wavefunction": wavefunction, "left_ops": left_ops, "right_ops": right_ops, "targets": targets}


def reference(wavefunction, left_ops, right_ops, targets):
    psi_wide = wavefunction.astype(jnp.float32)

    def one_operator(accumulated, op_item):
        left_block, right_block, target_ids = op_item
        middle = jnp.einsum("ab,vsbc->vsac", left_block.astype(jnp.float32), psi_wide).astype(jnp.bfloat16)
        contribution = jnp.einsum("vsac,dc->vsad", middle.astype(jnp.float32), right_block.astype(jnp.float32))
        return accumulated.at[:, target_ids].add(contribution), None

    start_value = jnp.zeros((NVEC, NSEC, SB, SB), jnp.float32)
    summed, _ = lax.scan(one_operator, start_value, (left_ops, right_ops, targets))
    return summed.astype(jnp.bfloat16)
```

```python
import functools

import jax
import jax.numpy as jnp
from jax import lax
from jax.experimental import pallas as pl
from jax.experimental.pallas import tpu as pltpu
from jax.sharding import PartitionSpec as P

F32 = jnp.float32
BF16 = jnp.bfloat16
MESH = pl.DeviceIdType.MESH
UNROLL = 4
HALF = 2


def kernel(psi_hbm, left_hbm, right_hbm, targets, out_ref, *scratch):
    vectors = psi_hbm.shape[0]
    ops, size, _ = left_hbm.shape
    sectors = targets.shape[1]
    chunks = vectors * HALF
    width = size // HALF
    rows_core = size // 2
    shard = rows_core // 4
    peers = 16
    rows_out = size // peers

    bufs = scratch[:chunks]
    (left, right, acc, own, sbuf, rbuf, s1_send, s1_recv, sh_send, sh_recv, mt_send, mt_recv,
     rs_send, rs_recv, load_sem, own_sem) = scratch[chunks:]

    op = lax.axis_index("op")
    sec = lax.axis_index("sec")
    core = lax.rem(op, 2)
    y = lax.rem(op // 2, 4)
    zl = op // 8
    x = lax.rem(sec, 4)
    zh = sec // 4

    def op_of(zl_, y_, core_):
        return zl_ * 8 + y_ * 2 + core_

    routes = ((2, 1, 7), (2, 0, 4), (1, 1, 6), (3, 1, 5), (1, 0, 2), (3, 0, 1), (0, 1, 3))

    def sec_peer(dx, dz):
        x_ = lax.rem(x + dx, 4)
        if dz:
            return op_of(1 - zl, y, core), (1 - zh) * 4 + x_
        return op, zh * 4 + x_

    near = (op_of(zl, lax.rem(y + 1, 4), core), op_of(zl, lax.rem(y + 3, 4), core), op_of(1 - zl, y, core))
    mate = op_of(zl, y, 1 - core)
    colour = lax.rem(y + 2 * zl, 4)
    base = core * rows_core

    def shard_rows(q):
        return pl.ds(pl.multiple_of(base + q * shard, 16), shard)

    barrier = pltpu.get_barrier_semaphore()
    for dx, dz, _ in routes:
        pl.semaphore_signal(barrier, inc=1, device_id=sec_peer(dx, dz), device_id_type=MESH)
    for j in range(1, peers):
        pl.semaphore_signal(barrier, inc=1, device_id=(lax.rem(op + j, peers), sec), device_id_type=MESH)
    own_copies = []
    for ch in range(chunks):
        v, h = divmod(ch, HALF)
        own_copies.append(pltpu.make_async_copy(
            psi_hbm.at[v, 0, :, h * width:(h + 1) * width], bufs[ch].at[0], own_sem.at[ch]))
        own_copies[-1].start()
    loads = [pltpu.make_async_copy(left_hbm, left, load_sem.at[0]),
             pltpu.make_async_copy(right_hbm, right, load_sem.at[1])]
    pl.semaphore_wait(barrier, len(routes) + peers - 1)

    first = []
    for ch in range(chunks):
        v, h = divmod(ch, HALF)
        for i, (dx, dz, slot) in enumerate(routes):
            rows = shard_rows(lax.rem(colour + 2 * dz, 4))
            first.append(pltpu.make_async_remote_copy(
                src_ref=psi_hbm.at[v, 0, rows, h * width:(h + 1) * width],
                dst_ref=bufs[ch].at[slot, rows, :],
                send_sem=s1_send.at[ch, i], recv_sem=s1_recv.at[ch, i],
                device_id=sec_peer(dx, dz), device_id_type=MESH))
    share = []
    for ch in range(chunks):
        rows = shard_rows(colour)
        for i in range(3):
            share.append(pltpu.make_async_remote_copy(
                src_ref=bufs[ch].at[1:8, rows, :], dst_ref=bufs[ch].at[1:8, rows, :],
                send_sem=sh_send.at[ch, i], recv_sem=sh_recv.at[ch, i],
                device_id=(near[i], sec), device_id_type=MESH))
    cross = []
    for ch in range(chunks):
        rows = pl.ds(pl.multiple_of(base, rows_core), rows_core)
        cross.append(pltpu.make_async_remote_copy(
            src_ref=bufs[ch].at[1:8, rows, :], dst_ref=bufs[ch].at[1:8, rows, :],
            send_sem=mt_send.at[ch], recv_sem=mt_recv.at[ch],
            device_id=(mate, sec), device_id_type=MESH))

    for copy in first[:len(routes)]:
        copy.start()
    for copy in loads:
        copy.start()
    for copy in first[len(routes):]:
        copy.start()

    def step_share(ch):
        for copy in first[ch * 7:ch * 7 + 7]:
            copy.wait_recv()
        for copy in share[ch * 3:ch * 3 + 3]:
            copy.start()

    def step_cross(ch):
        for copy in share[ch * 3:ch * 3 + 3]:
            copy.wait_recv()
        cross[ch].start()

    def step_ready(ch):
        cross[ch].wait_recv()
        own_copies[ch].wait()

    def slot_of(k):
        source = jnp.int32(0)
        for s in range(sectors):
            source = source + jnp.where(targets[k, s] == sec, s, 0)
        d = lax.rem(lax.rem(source, 4) - x + 4, 4)
        same = source // 4 == zh
        return jnp.where(same, jnp.where(d == 0, 0, jnp.where(d == 1, 1, jnp.where(d == 3, 2, 4))),
                         jnp.where(d == 0, 3, jnp.where(d == 1, 5, jnp.where(d == 3, 6, 7))))

    def compute(ch, start, stop):
        h = ch % HALF
        cols = slice(h * width, (h + 1) * width)

        def body(i, carry):
            mids = []
            for u in range(UNROLL):
                k = i * UNROLL + u
                mids.append(jnp.dot(left[k], bufs[ch][slot_of(k)], preferred_element_type=F32).astype(BF16))
            total = None
            for u in range(UNROLL):
                part = lax.dot_general(mids[u], right[i * UNROLL + u, :, cols], (((1,), (1,)), ((), ())),
                                       preferred_element_type=F32)
                total = part if total is None else total + part
            acc[...] += total
            return carry

        lax.fori_loop(start // UNROLL, stop // UNROLL, body, 0)

    def reduce_copies(v):
        copies = []
        for j in range(1, peers):
            to = lax.rem(op + j, peers)
            copies.append(pltpu.make_async_remote_copy(
                src_ref=sbuf.at[v, pl.ds(pl.multiple_of(to * rows_out, rows_out), rows_out), :],
                dst_ref=rbuf.at[v, j - 1],
                send_sem=rs_send.at[v, j - 1], recv_sem=rs_recv.at[v, j - 1],
                device_id=(to, sec), device_id_type=MESH))
        return copies

    reduces = []
    step_share(0)
    step_share(1)
    step_cross(0)
    for copy in loads:
        copy.wait()
    for ch in range(chunks):
        v, h = divmod(ch, HALF)
        step_ready(ch)
        if h == 0:
            acc[...] = jnp.zeros_like(acc)
        compute(ch, 0, ops // 2)
        if ch + 1 < chunks:
            step_cross(ch + 1)
        compute(ch, ops // 2, ops)
        if ch + 2 < chunks:
            step_share(ch + 2)
        if h == HALF - 1:
            sbuf[v] = acc[...].astype(BF16)
            own[v] = acc[pl.ds(pl.multiple_of(op * rows_out, rows_out), rows_out), :]
            reduces.append(reduce_copies(v))
            for copy in reduces[v]:
                copy.start()

    for v in range(vectors):
        for copy in reduces[v]:
            copy.wait_recv()
        total = own[v]
        for j in range(peers - 1):
            total = total + rbuf[v, j].astype(F32)
        out_ref[v, 0] = total.astype(BF16)

    for copy in first + share + cross:
        copy.wait_send()
    for copies in reduces:
        for copy in copies:
            copy.wait_send()


def per_device(wavefunction, left_ops, right_ops, targets):
    vectors, _, size, _ = wavefunction.shape
    ops = left_ops.shape[0]
    chunks = vectors * HALF
    width = size // HALF
    dma = pltpu.SemaphoreType.DMA
    scratch = [pltpu.VMEM((8, size, width), BF16) for _ in range(chunks)] + [
        pltpu.VMEM((ops, size, size), BF16),
        pltpu.VMEM((ops, size, size), BF16),
        pltpu.VMEM((size, size), F32),
        pltpu.VMEM((vectors, size // 16, size), F32),
        pltpu.VMEM((vectors, size, size), BF16),
        pltpu.VMEM((vectors, 15, size // 16, size), BF16),
        dma((chunks, 7)), dma((chunks, 7)), dma((chunks, 3)), dma((chunks, 3)), dma((chunks,)), dma((chunks,)),
        dma((vectors, 15)), dma((vectors, 15)), dma((2,)), dma((chunks,)),
    ]
    hbm = pl.BlockSpec(memory_space=pl.ANY)
    return pl.pallas_call(
        kernel,
        out_shape=jax.ShapeDtypeStruct((vectors, 1, size // 16, size), BF16),
        in_specs=[hbm, hbm, hbm, pl.BlockSpec(memory_space=pltpu.SMEM)],
        out_specs=pl.BlockSpec(memory_space=pltpu.VMEM),
        scratch_shapes=scratch,
        compiler_params=pltpu.CompilerParams(
            collective_id=0, has_side_effects=True, vmem_limit_bytes=62 * 2**20),
        name="sigma",
    )(wavefunction, left_ops, right_ops, targets)


def solution(mesh):
    return jax.shard_map(
        per_device,
        mesh=mesh,
        in_specs=(
            P(None, "sec", None, None),
            P("op", None, None),
            P("op", None, None),
            P("op", None),
        ),
        out_specs=P(None, "sec", "op", None),
        check_vma=False,
    )
```

```python
import jax
import jax.numpy as jnp
from jax import lax
from jax.experimental import pallas as pl
from jax.experimental.pallas import tpu as pltpu
from jax.sharding import PartitionSpec as P

F32 = jnp.float32
BF16 = jnp.bfloat16
MESH = pl.DeviceIdType.MESH
UNROLL = 4
HALF = 2
UNITS = 3


def kernel(psi_hbm, left_hbm, right_hbm, targets, out_ref, *scratch):
    vectors = psi_hbm.shape[0]
    ops, size, _ = left_hbm.shape
    sectors = targets.shape[1]
    width = size // HALF
    rows_core = size // 2
    shard = rows_core // 4
    peers = 16
    rows_out = size // peers
    chunks = 2 * HALF

    bufs = scratch[:chunks]
    (left, right, acc, sbuf, rbuf, s1_send, s1_recv, sh_send, sh_recv, mt_send, mt_recv,
     rs_send, rs_recv, load_sem, own_sem, self_sem) = scratch[chunks:]

    op = lax.axis_index("op")
    sec = lax.axis_index("sec")
    core = lax.rem(op, 2)
    y = lax.rem(op // 2, 4)
    zl = op // 8
    x = lax.rem(sec, 4)
    zh = sec // 4

    def op_of(zl_, y_, core_):
        return zl_ * 8 + y_ * 2 + core_

    def vector_a(d):
        return (3 * d + 1) // sectors

    def two_vectors(d):
        return jnp.logical_or(d == 2, d == 5)

    both = two_vectors(sec)
    units = (3 * sec + 1, jnp.where(sec == 5, 3 * sec + 2, 3 * sec), jnp.where(sec == 5, 3 * sec, 3 * sec + 2))
    unit_vector = [u // sectors for u in units]
    unit_target = [lax.rem(u, sectors) for u in units]

    routes = ((2, 1, 7), (2, 0, 4), (1, 1, 6), (3, 1, 5), (1, 0, 2), (3, 0, 1), (0, 1, 3))

    def sec_peer(dx, dz):
        x_ = lax.rem(x + dx, 4)
        if dz:
            return op_of(1 - zl, y, core), (1 - zh) * 4 + x_
        return op, zh * 4 + x_

    near = (op_of(zl, lax.rem(y + 1, 4), core), op_of(zl, lax.rem(y + 3, 4), core), op_of(1 - zl, y, core))
    mate = op_of(zl, y, 1 - core)
    colour = lax.rem(y + 2 * zl, 4)
    base = core * rows_core

    def shard_rows(q):
        return pl.ds(pl.multiple_of(base + q * shard, 16), shard)

    barrier = pltpu.get_barrier_semaphore()
    for dx, dz, _ in routes:
        pl.semaphore_signal(barrier, inc=1, device_id=sec_peer(dx, dz), device_id_type=MESH)
    for j in range(1, peers):
        pl.semaphore_signal(barrier, inc=1, device_id=(lax.rem(op + j, peers), sec), device_id_type=MESH)

    own_copies, first, share, cross = [], [], [], []
    for ch in range(chunks):
        is_b, h = divmod(ch, HALF)
        cols = slice(h * width, (h + 1) * width)
        own_copies.append(pltpu.make_async_copy(
            psi_hbm.at[1 if is_b else vector_a(sec), 0, :, cols], bufs[ch].at[0], own_sem.at[ch]))
        copies = []
        for i, (dx, dz, slot) in enumerate(routes):
            rows = shard_rows(lax.rem(colour + 2 * dz, 4))
            peer = sec_peer(dx, dz)
            copies.append((two_vectors(peer[1]) if is_b else None, pltpu.make_async_remote_copy(
                src_ref=psi_hbm.at[1 if is_b else vector_a(peer[1]), 0, rows, cols],
                dst_ref=bufs[ch].at[slot, rows, :],
                send_sem=s1_send.at[ch, i], recv_sem=s1_recv.at[ch, i],
                device_id=peer, device_id_type=MESH)))
        first.append(copies)
        rows = shard_rows(colour)
        share.append([pltpu.make_async_remote_copy(
            src_ref=bufs[ch].at[1:8, rows, :], dst_ref=bufs[ch].at[1:8, rows, :],
            send_sem=sh_send.at[ch, i], recv_sem=sh_recv.at[ch, i],
            device_id=(near[i], sec), device_id_type=MESH) for i in range(3)])
        rows = pl.ds(pl.multiple_of(base, rows_core), rows_core)
        cross.append(pltpu.make_async_remote_copy(
            src_ref=bufs[ch].at[1:8, rows, :], dst_ref=bufs[ch].at[1:8, rows, :],
            send_sem=mt_send.at[ch], recv_sem=mt_recv.at[ch],
            device_id=(mate, sec), device_id_type=MESH))
    loads = [pltpu.make_async_copy(left_hbm, left, load_sem.at[0]),
             pltpu.make_async_copy(right_hbm, right, load_sem.at[1])]

    def when(condition, action):
        if condition is None:
            action()
        else:
            pl.when(condition)(action)

    def start_first(ch):
        for condition, copy in first[ch]:
            when(condition, copy.start)

    def step_share(ch):
        for _, copy in first[ch]:
            copy.wait_recv()
        for copy in share[ch]:
            copy.start()

    def step_cross(ch):
        for copy in share[ch]:
            copy.wait_recv()
        cross[ch].start()

    def step_ready(ch):
        cross[ch].wait_recv()
        own_copies[ch].wait()

    own_copies[0].start()
    own_copies[1].start()
    for copy in loads:
        copy.start()
    pl.semaphore_wait(barrier, len(routes) + peers - 1)
    for ch in range(chunks):
        start_first(ch)

    @pl.when(both)
    def _():
        own_copies[2].start()
        own_copies[3].start()

    def slot_of(k, target):
        source = jnp.int32(0)
        for s in range(sectors):
            source = source + jnp.where(targets[k, s] == target, s, 0)
        d = lax.rem(lax.rem(source, 4) - x + 4, 4)
        same = source // 4 == zh
        return jnp.where(same, jnp.where(d == 0, 0, jnp.where(d == 1, 1, jnp.where(d == 3, 2, 4))),
                         jnp.where(d == 0, 3, jnp.where(d == 1, 5, jnp.where(d == 3, 6, 7))))

    def compute(unit, ch):
        h = ch % HALF
        cols = slice(h * width, (h + 1) * width)
        at = unit % 2

        def body(i, carry):
            mids = []
            for u in range(UNROLL):
                k = i * UNROLL + u
                mids.append(jnp.dot(left[k], bufs[ch][slot_of(k, unit_target[unit])],
                                    preferred_element_type=F32).astype(BF16))
            total = None
            for u in range(UNROLL):
                part = lax.dot_general(mids[u], right[i * UNROLL + u, :, cols], (((1,), (1,)), ((), ())),
                                       preferred_element_type=F32)
                total = part if total is None else total + part
            acc[at] += total
            return carry

        if h == 0:
            acc[at] = jnp.zeros((size, size), F32)
        lax.fori_loop(0, ops // UNROLL, body, 0)

    def out_rows(to):
        return pl.ds(pl.multiple_of(to * rows_out, rows_out), rows_out)

    def reduce_copy(unit, j):
        to = lax.rem(op + j, peers)
        return pltpu.make_async_remote_copy(
            src_ref=sbuf.at[unit, out_rows(to), :],
            dst_ref=rbuf.at[unit_vector[unit], op],
            send_sem=rs_send.at[unit, j], recv_sem=rs_recv.at[unit_vector[unit], op],
            device_id=(to, unit_target[unit]), device_id_type=MESH)

    def keep_copy(unit):
        return pltpu.make_async_copy(sbuf.at[unit, out_rows(op), :], rbuf.at[unit_vector[unit], op], self_sem.at[0])

    def send(unit):
        sbuf[unit] = acc[unit % 2].astype(BF16)
        for j in range(1, peers):
            reduce_copy(unit, j).start()
        mine = unit_target[unit] == sec
        pl.when(jnp.logical_not(mine))(lambda: reduce_copy(unit, 0).start())
        pl.when(mine)(lambda: keep_copy(unit).start())

    step_share(0)
    step_share(1)
    step_cross(0)
    for copy in loads:
        copy.wait()
    step_ready(0)
    compute(0, 0)
    step_cross(1)

    @pl.when(both)
    def _():
        step_share(2)
        step_share(3)

    compute(1, 0)
    step_ready(1)
    compute(0, 1)
    send(0)
    pl.when(both)(lambda: step_cross(2))
    compute(1, 1)
    send(1)

    @pl.when(both)
    def _():
        step_cross(3)
        step_ready(2)
        compute(2, 2)
        step_ready(3)
        compute(2, 3)

    @pl.when(jnp.logical_not(both))
    def _():
        compute(2, 0)
        compute(2, 1)

    send(2)

    for unit in range(UNITS):
        pl.when(unit_target[unit] == sec)(lambda: keep_copy(unit).wait())
    for v in range(vectors):
        def arrival(j):
            source = lax.rem(op + j, peers)
            return pltpu.make_async_remote_copy(
                src_ref=sbuf.at[0, out_rows(op), :], dst_ref=rbuf.at[v, source],
                send_sem=rs_send.at[0, j], recv_sem=rs_recv.at[v, source],
                device_id=(source, sec), device_id_type=MESH)

        pl.when((sectors * v + sec) // UNITS != sec)(lambda: arrival(0).wait_recv())
        for j in range(1, peers):
            arrival(j).wait_recv()
        total = rbuf[v, 0].astype(F32)
        for j in range(1, peers):
            total = total + rbuf[v, j].astype(F32)
        out_ref[v, 0] = total.astype(BF16)

    for ch in range(chunks):
        for condition, copy in first[ch]:
            when(condition, copy.wait_send)

        def sent():
            for copy in share[ch] + [cross[ch]]:
                copy.wait_send()

        when(both if ch >= HALF else None, sent)
    for unit in range(UNITS):
        for j in range(1, peers):
            reduce_copy(unit, j).wait_send()
        pl.when(unit_target[unit] != sec)(lambda: reduce_copy(unit, 0).wait_send())


def per_device(wavefunction, left_ops, right_ops, targets):
    vectors, _, size, _ = wavefunction.shape
    ops = left_ops.shape[0]
    chunks = 2 * HALF
    width = size // HALF
    dma = pltpu.SemaphoreType.DMA
    scratch = [pltpu.VMEM((8, size, width), BF16) for _ in range(chunks)] + [
        pltpu.VMEM((ops, size, size), BF16),
        pltpu.VMEM((ops, size, size), BF16),
        pltpu.VMEM((2, size, size), F32),
        pltpu.VMEM((UNITS, size, size), BF16),
        pltpu.VMEM((vectors, 16, size // 16, size), BF16),
        dma((chunks, 7)), dma((chunks, 7)), dma((chunks, 3)), dma((chunks, 3)), dma((chunks,)), dma((chunks,)),
        dma((UNITS, 16)), dma((vectors, 16)), dma((2,)), dma((chunks,)), dma((1,)),
    ]
    hbm = pl.BlockSpec(memory_space=pl.ANY)
    return pl.pallas_call(
        kernel,
        out_shape=jax.ShapeDtypeStruct((vectors, 1, size // 16, size), BF16),
        in_specs=[hbm, hbm, hbm, pl.BlockSpec(memory_space=pltpu.SMEM)],
        out_specs=pl.BlockSpec(memory_space=pltpu.VMEM),
        scratch_shapes=scratch,
        compiler_params=pltpu.CompilerParams(
            collective_id=0, has_side_effects=True, vmem_limit_bytes=62 * 2**20),
        name="sigma",
    )(wavefunction, left_ops, right_ops, targets)


def solution(mesh):
    return jax.shard_map(
        per_device,
        mesh=mesh,
        in_specs=(
            P(None, "sec", None, None),
            P("op", None, None),
            P("op", None, None),
            P("op", None),
        ),
        out_specs=P(None, "sec", "op", None),
        check_vma=False,
    )
```

```python
import jax
import jax.numpy as jnp
from jax import lax
from jax.experimental import pallas as pl
from jax.experimental.pallas import tpu as pltpu
from jax.sharding import PartitionSpec as P

F32 = jnp.float32
BF16 = jnp.bfloat16
MESH = pl.DeviceIdType.MESH
UNROLL = 4
HALF = 2
UNITS = 3


def kernel(psi_hbm, left_hbm, right_hbm, targets, out_ref, *scratch):
    vectors = psi_hbm.shape[0]
    ops, size, _ = left_hbm.shape
    sectors = targets.shape[1]
    width = size // HALF
    rows_core = size // 2
    shard = rows_core // 4
    peers = 16
    chips = peers // 2
    rows_out = size // peers
    chunks = 2 * HALF

    bufs = scratch[:chunks]
    (left, right, acc, sbuf, mbuf, tbuf, rbuf, s1_send, s1_recv, sh_send, sh_recv, mt_send, mt_recv,
     pr_send, pr_recv, rs_send, rs_recv, load_sem, own_sem, self_sem) = scratch[chunks:]

    op = lax.axis_index("op")
    sec = lax.axis_index("sec")
    core = lax.rem(op, 2)
    y = lax.rem(op // 2, 4)
    zl = op // 8
    x = lax.rem(sec, 4)
    zh = sec // 4

    def op_of(zl_, y_, core_):
        return zl_ * 8 + y_ * 2 + core_

    def vector_a(d):
        return (3 * d + 1) // sectors

    def two_vectors(d):
        return jnp.logical_or(d == 2, d == 5)

    both = two_vectors(sec)
    units = (3 * sec + 1, jnp.where(sec == 5, 3 * sec + 2, 3 * sec), jnp.where(sec == 5, 3 * sec, 3 * sec + 2))
    unit_vector = [u // sectors for u in units]
    unit_target = [lax.rem(u, sectors) for u in units]

    routes = ((2, 1, 7), (2, 0, 4), (1, 1, 6), (3, 1, 5), (1, 0, 2), (3, 0, 1), (0, 1, 3))

    def sec_peer(dx, dz):
        x_ = lax.rem(x + dx, 4)
        if dz:
            return op_of(1 - zl, y, core), (1 - zh) * 4 + x_
        return op, zh * 4 + x_

    near = (op_of(zl, lax.rem(y + 1, 4), core), op_of(zl, lax.rem(y + 3, 4), core), op_of(1 - zl, y, core))
    mate = op_of(zl, y, 1 - core)
    colour = lax.rem(y + 2 * zl, 4)
    base = core * rows_core

    def shard_rows(q):
        return pl.ds(pl.multiple_of(base + q * shard, 16), shard)

    barrier = pltpu.get_barrier_semaphore()
    for dx, dz, _ in routes:
        pl.semaphore_signal(barrier, inc=1, device_id=sec_peer(dx, dz), device_id_type=MESH)
    for j in range(1, peers):
        pl.semaphore_signal(barrier, inc=1, device_id=(lax.rem(op + j, peers), sec), device_id_type=MESH)

    own_copies, first, share, cross = [], [], [], []
    for ch in range(chunks):
        is_b, h = divmod(ch, HALF)
        cols = slice(h * width, (h + 1) * width)
        own_copies.append(pltpu.make_async_copy(
            psi_hbm.at[1 if is_b else vector_a(sec), 0, :, cols], bufs[ch].at[0], own_sem.at[ch]))
        copies = []
        for i, (dx, dz, slot) in enumerate(routes):
            rows = shard_rows(lax.rem(colour + 2 * dz, 4))
            peer = sec_peer(dx, dz)
            copies.append((two_vectors(peer[1]) if is_b else None, pltpu.make_async_remote_copy(
                src_ref=psi_hbm.at[1 if is_b else vector_a(peer[1]), 0, rows, cols],
                dst_ref=bufs[ch].at[slot, rows, :],
                send_sem=s1_send.at[ch, i], recv_sem=s1_recv.at[ch, i],
                device_id=peer, device_id_type=MESH)))
        first.append(copies)
        rows = shard_rows(colour)
        share.append([pltpu.make_async_remote_copy(
            src_ref=bufs[ch].at[1:8, rows, :], dst_ref=bufs[ch].at[1:8, rows, :],
            send_sem=sh_send.at[ch, i], recv_sem=sh_recv.at[ch, i],
            device_id=(near[i], sec), device_id_type=MESH) for i in range(3)])
        rows = pl.ds(pl.multiple_of(base, rows_core), rows_core)
        cross.append(pltpu.make_async_remote_copy(
            src_ref=bufs[ch].at[1:8, rows, :], dst_ref=bufs[ch].at[1:8, rows, :],
            send_sem=mt_send.at[ch], recv_sem=mt_recv.at[ch],
            device_id=(mate, sec), device_id_type=MESH))
    loads = [pltpu.make_async_copy(left_hbm, left, load_sem.at[0]),
             pltpu.make_async_copy(right_hbm, right, load_sem.at[1])]

    def when(condition, action):
        if condition is None:
            action()
        else:
            pl.when(condition)(action)

    def start_first(ch):
        for condition, copy in first[ch]:
            when(condition, copy.start)

    def step_share(ch):
        for _, copy in first[ch]:
            copy.wait_recv()
        for copy in share[ch]:
            copy.start()

    def step_cross(ch):
        for copy in share[ch]:
            copy.wait_recv()
        cross[ch].start()

    def step_ready(ch):
        cross[ch].wait_recv()
        own_copies[ch].wait()

    own_copies[0].start()
    own_copies[1].start()
    for copy in loads:
        copy.start()
    pl.semaphore_wait(barrier, len(routes) + peers - 1)
    for ch in range(chunks):
        start_first(ch)

    @pl.when(both)
    def _():
        own_copies[2].start()
        own_copies[3].start()

    def slot_of(k, target):
        source = jnp.int32(0)
        for s in range(sectors):
            source = source + jnp.where(targets[k, s] == target, s, 0)
        d = lax.rem(lax.rem(source, 4) - x + 4, 4)
        same = source // 4 == zh
        return jnp.where(same, jnp.where(d == 0, 0, jnp.where(d == 1, 1, jnp.where(d == 3, 2, 4))),
                         jnp.where(d == 0, 3, jnp.where(d == 1, 5, jnp.where(d == 3, 6, 7))))

    def compute(unit, ch, start=0, stop=None):
        h = ch % HALF
        cols = slice(h * width, (h + 1) * width)
        at = unit

        def body(i, carry):
            mids = []
            for u in range(UNROLL):
                k = i * UNROLL + u
                mids.append(jnp.dot(left[k], bufs[ch][slot_of(k, unit_target[unit])],
                                    preferred_element_type=F32).astype(BF16))
            total = None
            for u in range(UNROLL):
                part = lax.dot_general(mids[u], right[i * UNROLL + u, :, cols], (((1,), (1,)), ((), ())),
                                       preferred_element_type=F32)
                total = part if total is None else total + part
            acc[at] += total.reshape(chips, 2, rows_out, size)
            return carry

        if h == 0 and start == 0:
            acc[at] = jnp.zeros(acc.shape[1:], F32)
        lax.fori_loop(start // UNROLL, (ops if stop is None else stop) // UNROLL, body, 0)

    chip = op // 2

    def pair_copy(unit):
        return pltpu.make_async_remote_copy(
            src_ref=sbuf.at[unit], dst_ref=mbuf.at[unit],
            send_sem=pr_send.at[unit], recv_sem=pr_recv.at[unit],
            device_id=(mate, sec), device_id_type=MESH)

    def reduce_copy(unit, j):
        to = lax.rem(chip + j, chips)
        return pltpu.make_async_remote_copy(
            src_ref=tbuf.at[unit, to],
            dst_ref=rbuf.at[unit_vector[unit], chip],
            send_sem=rs_send.at[unit, j], recv_sem=rs_recv.at[unit_vector[unit], chip],
            device_id=(2 * to + core, unit_target[unit]), device_id_type=MESH)

    def keep_copy(unit):
        return pltpu.make_async_copy(tbuf.at[unit, chip], rbuf.at[unit_vector[unit], chip], self_sem.at[0])

    def send_pair(unit):
        sbuf[unit] = acc[unit, :, 1 - core].astype(BF16)
        pair_copy(unit).start()

    def send(unit):
        pair_copy(unit).wait_recv()
        tbuf[unit] = (acc[unit, :, core] + mbuf[unit].astype(F32)).astype(BF16)
        for j in (4, 5, 3, 6, 2, 7, 1):
            reduce_copy(unit, j).start()
        mine = unit_target[unit] == sec
        pl.when(jnp.logical_not(mine))(lambda: reduce_copy(unit, 0).start())
        pl.when(mine)(lambda: keep_copy(unit).start())

    step_share(0)
    step_share(1)
    step_cross(0)
    for copy in loads:
        copy.wait()
    step_ready(0)
    compute(0, 0)
    step_cross(1)

    @pl.when(both)
    def _():
        step_share(2)
        step_share(3)

    compute(1, 0)
    step_ready(1)
    compute(0, 1)
    send_pair(0)
    pl.when(both)(lambda: step_cross(2))
    compute(1, 1, 0, ops // 2)
    send(0)
    compute(1, 1, ops // 2)
    send_pair(1)

    @pl.when(both)
    def _():
        step_cross(3)
        step_ready(2)
        compute(2, 2)
        send(1)
        step_ready(3)
        compute(2, 3)

    @pl.when(jnp.logical_not(both))
    def _():
        compute(2, 0)
        send(1)
        compute(2, 1)

    send_pair(2)
    send(2)

    for unit in range(UNITS):
        pl.when(unit_target[unit] == sec)(lambda: keep_copy(unit).wait())
    for v in range(vectors):
        def arrival(j):
            source = lax.rem(chip + j, chips)
            return pltpu.make_async_remote_copy(
                src_ref=tbuf.at[0, chip], dst_ref=rbuf.at[v, source],
                send_sem=rs_send.at[0, j], recv_sem=rs_recv.at[v, source],
                device_id=(2 * source + core, sec), device_id_type=MESH)

        pl.when((sectors * v + sec) // UNITS != sec)(lambda: arrival(0).wait_recv())
        for j in range(1, chips):
            arrival(j).wait_recv()
        total = rbuf[v, 0].astype(F32)
        for j in range(1, chips):
            total = total + rbuf[v, j].astype(F32)
        out_ref[v, 0] = total.astype(BF16)

    for ch in range(chunks):
        for condition, copy in first[ch]:
            when(condition, copy.wait_send)

        def sent():
            for copy in share[ch] + [cross[ch]]:
                copy.wait_send()

        when(both if ch >= HALF else None, sent)
    for unit in range(UNITS):
        pair_copy(unit).wait_send()
        for j in range(1, chips):
            reduce_copy(unit, j).wait_send()
        pl.when(unit_target[unit] != sec)(lambda: reduce_copy(unit, 0).wait_send())


def per_device(wavefunction, left_ops, right_ops, targets):
    vectors, _, size, _ = wavefunction.shape
    ops = left_ops.shape[0]
    chunks = 2 * HALF
    width = size // HALF
    dma = pltpu.SemaphoreType.DMA
    scratch = [pltpu.VMEM((8, size, width), BF16) for _ in range(chunks)] + [
        pltpu.VMEM((ops, size, size), BF16),
        pltpu.VMEM((ops, size, size), BF16),
        pltpu.VMEM((UNITS, 8, 2, size // 16, size), F32),
        pltpu.VMEM((UNITS, 8, size // 16, size), BF16),
        pltpu.VMEM((UNITS, 8, size // 16, size), BF16),
        pltpu.VMEM((UNITS, 8, size // 16, size), BF16),
        pltpu.VMEM((vectors, 8, size // 16, size), BF16),
        dma((chunks, 7)), dma((chunks, 7)), dma((chunks, 3)), dma((chunks, 3)), dma((chunks,)), dma((chunks,)),
        dma((UNITS,)), dma((UNITS,)), dma((UNITS, 8)), dma((vectors, 8)), dma((2,)), dma((chunks,)), dma((1,)),
    ]
    hbm = pl.BlockSpec(memory_space=pl.ANY)
    return pl.pallas_call(
        kernel,
        out_shape=jax.ShapeDtypeStruct((vectors, 1, size // 16, size), BF16),
        in_specs=[hbm, hbm, hbm, pl.BlockSpec(memory_space=pltpu.SMEM)],
        out_specs=pl.BlockSpec(memory_space=pltpu.VMEM),
        scratch_shapes=scratch,
        compiler_params=pltpu.CompilerParams(
            collective_id=0, has_side_effects=True, vmem_limit_bytes=62 * 2**20),
        name="sigma",
    )(wavefunction, left_ops, right_ops, targets)


def solution(mesh):
    return jax.shard_map(
        per_device,
        mesh=mesh,
        in_specs=(
            P(None, "sec", None, None),
            P("op", None, None),
            P("op", None, None),
            P("op", None),
        ),
        out_specs=P(None, "sec", "op", None),
        check_vma=False,
    )
```

```python
import jax
import jax.numpy as jnp
from jax import lax
from jax.experimental import pallas as pl
from jax.experimental.pallas import tpu as pltpu
from jax.sharding import PartitionSpec as P

F32 = jnp.float32
BF16 = jnp.bfloat16
MESH = pl.DeviceIdType.MESH
UNROLL = 4
HALF = 2
UNITS = 3
SPLIT = 2


def kernel(psi_hbm, left_hbm, right_hbm, targets, out_ref, *scratch):
    vectors = psi_hbm.shape[0]
    ops, size, _ = left_hbm.shape
    sectors = targets.shape[1]
    width = size // HALF
    rows_core = size // 2
    shard = rows_core // 4
    peers = 16
    chips = peers // 2
    rows_out = size // peers
    chunks = 2 * HALF

    bufs = scratch[:chunks]
    (left, right, acc, sbuf, mbuf, tbuf, rbuf, s1_send, s1_recv, sh_send, sh_recv, mt_send, mt_recv,
     pr_send, pr_recv, rs_send, rs_recv, load_sem, own_sem, self_sem) = scratch[chunks:]

    op = lax.axis_index("op")
    sec = lax.axis_index("sec")
    core = lax.rem(op, 2)
    y = lax.rem(op // 2, 4)
    zl = op // 8
    x = lax.rem(sec, 4)
    zh = sec // 4

    def op_of(zl_, y_, core_):
        return zl_ * 8 + y_ * 2 + core_

    def vector_a(d):
        return (3 * d + 1) // sectors

    def two_vectors(d):
        return jnp.logical_or(d == 2, d == 5)

    both = two_vectors(sec)
    units = (3 * sec + 1, jnp.where(sec == 5, 3 * sec + 2, 3 * sec), jnp.where(sec == 5, 3 * sec, 3 * sec + 2))
    unit_vector = [u // sectors for u in units]
    unit_target = [lax.rem(u, sectors) for u in units]

    routes = ((2, 1, 7), (2, 0, 4), (1, 1, 6), (3, 1, 5), (1, 0, 2), (3, 0, 1), (0, 1, 3))

    def sec_peer(dx, dz):
        x_ = lax.rem(x + dx, 4)
        if dz:
            return op_of(1 - zl, y, core), (1 - zh) * 4 + x_
        return op, zh * 4 + x_

    near = (op_of(zl, lax.rem(y + 1, 4), core), op_of(zl, lax.rem(y + 3, 4), core), op_of(1 - zl, y, core))
    mate = op_of(zl, y, 1 - core)
    colour = lax.rem(y + 2 * zl, 4)
    base = core * rows_core

    piece = shard // SPLIT

    def shard_rows(q, g):
        return pl.ds(pl.multiple_of(base + lax.rem(q, 4) * shard + g * piece, 16), piece)

    barrier = pltpu.get_barrier_semaphore()
    for dx, dz, _ in routes:
        pl.semaphore_signal(barrier, inc=1, device_id=sec_peer(dx, dz), device_id_type=MESH)
    for j in range(1, peers):
        pl.semaphore_signal(barrier, inc=1, device_id=(lax.rem(op + j, peers), sec), device_id_type=MESH)

    own_copies, first, share, cross = [], [], [], []
    for ch in range(chunks):
        is_b, h = divmod(ch, HALF)
        cols = slice(h * width, (h + 1) * width)
        own_copies.append(pltpu.make_async_copy(
            psi_hbm.at[1 if is_b else vector_a(sec), 0, :, cols], bufs[ch].at[0], own_sem.at[ch]))
        first.append([])
        share.append([])
        cross.append([])
        for g in range(SPLIT):
            copies = []
            for i, (dx, dz, slot) in enumerate(routes):
                rows = shard_rows(colour + 2 * dz, g)
                peer = sec_peer(dx, dz)
                copies.append((two_vectors(peer[1]) if is_b else None, pltpu.make_async_remote_copy(
                    src_ref=psi_hbm.at[1 if is_b else vector_a(peer[1]), 0, rows, cols],
                    dst_ref=bufs[ch].at[slot, rows, :],
                    send_sem=s1_send.at[ch, g, i], recv_sem=s1_recv.at[ch, g, i],
                    device_id=peer, device_id_type=MESH)))
            first[ch].append(copies)
            rows = shard_rows(colour, g)
            share[ch].append([pltpu.make_async_remote_copy(
                src_ref=bufs[ch].at[1:8, rows, :], dst_ref=bufs[ch].at[1:8, rows, :],
                send_sem=sh_send.at[ch, g, i], recv_sem=sh_recv.at[ch, g, i],
                device_id=(near[i], sec), device_id_type=MESH) for i in range(3)])
            copies = []
            for n, q in enumerate((0, 3, 1, 2)):
                rows = shard_rows(colour + q, g)
                copies.append(pltpu.make_async_remote_copy(
                    src_ref=bufs[ch].at[1:8, rows, :], dst_ref=bufs[ch].at[1:8, rows, :],
                    send_sem=mt_send.at[ch, g, n], recv_sem=mt_recv.at[ch, g, n],
                    device_id=(mate, sec), device_id_type=MESH))
            cross[ch].append(copies)
    loads = [pltpu.make_async_copy(left_hbm, left, load_sem.at[0]),
             pltpu.make_async_copy(right_hbm, right, load_sem.at[1])]

    def when(condition, action):
        if condition is None:
            action()
        else:
            pl.when(condition)(action)

    def start_first(ch):
        for g in range(SPLIT):
            for condition, copy in first[ch][g]:
                when(condition, copy.start)

    def step_share(ch, g):
        for _, copy in first[ch][g]:
            copy.wait_recv()
        for copy in share[ch][g]:
            copy.start()
        cross[ch][g][0].start()

    def step_cross(ch, g):
        for i in range(3):
            share[ch][g][i].wait_recv()
            cross[ch][g][i + 1].start()

    def step_ready(ch):
        for copies in cross[ch]:
            for copy in copies:
                copy.wait_recv()
        own_copies[ch].wait()

    own_copies[0].start()
    own_copies[1].start()
    for copy in loads:
        copy.start()
    pl.semaphore_wait(barrier, len(routes) + peers - 1)
    start_first(0)
    start_first(1)

    def slot_of(k, target):
        source = jnp.int32(0)
        for s in range(sectors):
            source = source + jnp.where(targets[k, s] == target, s, 0)
        d = lax.rem(lax.rem(source, 4) - x + 4, 4)
        same = source // 4 == zh
        return jnp.where(same, jnp.where(d == 0, 0, jnp.where(d == 1, 1, jnp.where(d == 3, 2, 4))),
                         jnp.where(d == 0, 3, jnp.where(d == 1, 5, jnp.where(d == 3, 6, 7))))

    def compute(unit, ch, start=0, stop=None):
        h = ch % HALF
        cols = slice(h * width, (h + 1) * width)
        at = unit

        def body(i, carry):
            mids = []
            for u in range(UNROLL):
                k = i * UNROLL + u
                mids.append(jnp.dot(left[k], bufs[ch][slot_of(k, unit_target[unit])],
                                    preferred_element_type=F32).astype(BF16))
            total = None
            for u in range(UNROLL):
                part = lax.dot_general(mids[u], right[i * UNROLL + u, :, cols], (((1,), (1,)), ((), ())),
                                       preferred_element_type=F32)
                total = part if total is None else total + part
            acc[at] += total.reshape(chips, 2, rows_out, size)
            return carry

        if h == 0 and start == 0:
            acc[at] = jnp.zeros(acc.shape[1:], F32)
        lax.fori_loop(start // UNROLL, (ops if stop is None else stop) // UNROLL, body, 0)

    chip = op // 2

    def pair_copy(unit):
        return pltpu.make_async_remote_copy(
            src_ref=sbuf.at[unit], dst_ref=mbuf.at[unit],
            send_sem=pr_send.at[unit], recv_sem=pr_recv.at[unit],
            device_id=(mate, sec), device_id_type=MESH)

    def reduce_copy(unit, j):
        to = lax.rem(chip + j, chips)
        return pltpu.make_async_remote_copy(
            src_ref=tbuf.at[unit, to],
            dst_ref=rbuf.at[unit_vector[unit], chip],
            send_sem=rs_send.at[unit, j], recv_sem=rs_recv.at[unit_vector[unit], chip],
            device_id=(2 * to + core, unit_target[unit]), device_id_type=MESH)

    def keep_copy(unit):
        return pltpu.make_async_copy(tbuf.at[unit, chip], rbuf.at[unit_vector[unit], chip], self_sem.at[0])

    def send_pair(unit):
        sbuf[unit] = acc[unit, :, 1 - core].astype(BF16)
        pair_copy(unit).start()

    def send(unit):
        pair_copy(unit).wait_recv()
        tbuf[unit] = (acc[unit, :, core] + mbuf[unit].astype(F32)).astype(BF16)
        for j in (4, 5, 3, 6, 2, 7, 1):
            reduce_copy(unit, j).start()
        mine = unit_target[unit] == sec
        pl.when(jnp.logical_not(mine))(lambda: reduce_copy(unit, 0).start())
        pl.when(mine)(lambda: keep_copy(unit).start())

    step_share(0, 0)
    step_share(0, 1)
    step_share(1, 0)
    step_cross(0, 0)
    step_share(1, 1)
    step_cross(0, 1)
    start_first(2)
    start_first(3)

    @pl.when(both)
    def _():
        own_copies[2].start()
        own_copies[3].start()

    for copy in loads:
        copy.wait()
    step_ready(0)
    compute(0, 0)
    for g in range(SPLIT):
        step_cross(1, g)

    @pl.when(both)
    def _():
        for ch in (2, 3):
            for g in range(SPLIT):
                step_share(ch, g)

    compute(1, 0)
    step_ready(1)
    compute(0, 1)
    send_pair(0)

    @pl.when(both)
    def _():
        for g in range(SPLIT):
            step_cross(2, g)

    compute(1, 1, 0, ops // 2)
    send(0)
    compute(1, 1, ops // 2)
    send_pair(1)

    @pl.when(both)
    def _():
        for g in range(SPLIT):
            step_cross(3, g)
        step_ready(2)
        compute(2, 2)
        send(1)
        step_ready(3)
        compute(2, 3)

    @pl.when(jnp.logical_not(both))
    def _():
        compute(2, 0)
        send(1)
        compute(2, 1)

    send_pair(2)
    send(2)

    for unit in range(UNITS):
        pl.when(unit_target[unit] == sec)(lambda: keep_copy(unit).wait())
    for v in range(vectors):
        def arrival(j):
            source = lax.rem(chip + j, chips)
            return pltpu.make_async_remote_copy(
                src_ref=tbuf.at[0, chip], dst_ref=rbuf.at[v, source],
                send_sem=rs_send.at[0, j], recv_sem=rs_recv.at[v, source],
                device_id=(2 * source + core, sec), device_id_type=MESH)

        pl.when((sectors * v + sec) // UNITS != sec)(lambda: arrival(0).wait_recv())
        for j in range(1, chips):
            arrival(j).wait_recv()
        total = rbuf[v, 0].astype(F32)
        for j in range(1, chips):
            total = total + rbuf[v, j].astype(F32)
        out_ref[v, 0] = total.astype(BF16)

    for ch in range(chunks):
        for g in range(SPLIT):
            for condition, copy in first[ch][g]:
                when(condition, copy.wait_send)

        def sent():
            for g in range(SPLIT):
                for copy in share[ch][g] + cross[ch][g]:
                    copy.wait_send()

        when(both if ch >= HALF else None, sent)
    for unit in range(UNITS):
        pair_copy(unit).wait_send()
        for j in range(1, chips):
            reduce_copy(unit, j).wait_send()
        pl.when(unit_target[unit] != sec)(lambda: reduce_copy(unit, 0).wait_send())


def per_device(wavefunction, left_ops, right_ops, targets):
    vectors, _, size, _ = wavefunction.shape
    ops = left_ops.shape[0]
    chunks = 2 * HALF
    width = size // HALF
    dma = pltpu.SemaphoreType.DMA
    scratch = [pltpu.VMEM((8, size, width), BF16) for _ in range(chunks)] + [
        pltpu.VMEM((ops, size, size), BF16),
        pltpu.VMEM((ops, size, size), BF16),
        pltpu.VMEM((UNITS, 8, 2, size // 16, size), F32),
        pltpu.VMEM((UNITS, 8, size // 16, size), BF16),
        pltpu.VMEM((UNITS, 8, size // 16, size), BF16),
        pltpu.VMEM((UNITS, 8, size // 16, size), BF16),
        pltpu.VMEM((vectors, 8, size // 16, size), BF16),
        dma((chunks, SPLIT, 7)), dma((chunks, SPLIT, 7)), dma((chunks, SPLIT, 3)), dma((chunks, SPLIT, 3)),
        dma((chunks, SPLIT, 4)), dma((chunks, SPLIT, 4)),
        dma((UNITS,)), dma((UNITS,)), dma((UNITS, 8)), dma((vectors, 8)), dma((2,)), dma((chunks,)), dma((1,)),
    ]
    hbm = pl.BlockSpec(memory_space=pl.ANY)
    return pl.pallas_call(
        kernel,
        out_shape=jax.ShapeDtypeStruct((vectors, 1, size // 16, size), BF16),
        in_specs=[hbm, hbm, hbm, pl.BlockSpec(memory_space=pltpu.SMEM)],
        out_specs=pl.BlockSpec(memory_space=pltpu.VMEM),
        scratch_shapes=scratch,
        compiler_params=pltpu.CompilerParams(
            collective_id=0, has_side_effects=True, vmem_limit_bytes=62 * 2**20),
        name="sigma",
    )(wavefunction, left_ops, right_ops, targets)


def solution(mesh):
    return jax.shard_map(
        per_device,
        mesh=mesh,
        in_specs=(
            P(None, "sec", None, None),
            P("op", None, None),
            P("op", None, None),
            P("op", None),
        ),
        out_specs=P(None, "sec", "op", None),
        check_vma=False,
    )
```

```python
import jax
import jax.numpy as jnp
from jax import lax
from jax.experimental import pallas as pl
from jax.experimental.pallas import tpu as pltpu
from jax.sharding import PartitionSpec as P

F32 = jnp.float32
BF16 = jnp.bfloat16
MESH = pl.DeviceIdType.MESH
UNROLL = 8
HALF = 2
UNITS = 3
SPLIT = 2


def kernel(psi_hbm, left_hbm, right_hbm, targets, out_ref, *scratch):
    vectors = psi_hbm.shape[0]
    ops, size, _ = left_hbm.shape
    sectors = targets.shape[1]
    width = size // HALF
    rows_core = size // 2
    shard = rows_core // 4
    peers = 16
    chips = peers // 2
    rows_out = size // peers
    chunks = 2 * HALF

    bufs = scratch[:chunks]
    (left, right, acc, sbuf, mbuf, tbuf, rbuf, s1_send, s1_recv, sh_send, sh_recv, mt_send, mt_recv,
     pr_send, pr_recv, rs_send, rs_recv, load_sem, own_sem, self_sem) = scratch[chunks:]

    op = lax.axis_index("op")
    sec = lax.axis_index("sec")
    core = lax.rem(op, 2)
    y = lax.rem(op // 2, 4)
    zl = op // 8
    x = lax.rem(sec, 4)
    zh = sec // 4

    def op_of(zl_, y_, core_):
        return zl_ * 8 + y_ * 2 + core_

    def vector_a(d):
        return (3 * d + 1) // sectors

    def two_vectors(d):
        return jnp.logical_or(d == 2, d == 5)

    both = two_vectors(sec)
    units = (3 * sec + 1, jnp.where(sec == 5, 3 * sec + 2, 3 * sec), jnp.where(sec == 5, 3 * sec, 3 * sec + 2))
    unit_vector = [u // sectors for u in units]
    unit_target = [lax.rem(u, sectors) for u in units]

    routes = ((2, 1, 7), (2, 0, 4), (1, 1, 6), (3, 1, 5), (1, 0, 2), (3, 0, 1), (0, 1, 3))

    def sec_peer(dx, dz):
        x_ = lax.rem(x + dx, 4)
        if dz:
            return op_of(1 - zl, y, core), (1 - zh) * 4 + x_
        return op, zh * 4 + x_

    near = (op_of(zl, lax.rem(y + 1, 4), core), op_of(zl, lax.rem(y + 3, 4), core), op_of(1 - zl, y, core))
    mate = op_of(zl, y, 1 - core)
    colour = lax.rem(y + 2 * zl, 4)
    base = core * rows_core

    piece = shard // SPLIT

    def shard_rows(q, g):
        return pl.ds(pl.multiple_of(base + lax.rem(q, 4) * shard + g * piece, 16), piece)

    barrier = pltpu.get_barrier_semaphore()
    for dx, dz, _ in routes:
        pl.semaphore_signal(barrier, inc=1, device_id=sec_peer(dx, dz), device_id_type=MESH)
    for j in range(1, peers):
        pl.semaphore_signal(barrier, inc=1, device_id=(lax.rem(op + j, peers), sec), device_id_type=MESH)

    own_copies, first, share, cross = [], [], [], []
    for ch in range(chunks):
        is_b, h = divmod(ch, HALF)
        cols = slice(h * width, (h + 1) * width)
        own_copies.append(pltpu.make_async_copy(
            psi_hbm.at[1 if is_b else vector_a(sec), 0, :, cols], bufs[ch].at[0], own_sem.at[ch]))
        first.append([])
        share.append([])
        cross.append([])
        for g in range(SPLIT):
            copies = []
            for i, (dx, dz, slot) in enumerate(routes):
                rows = shard_rows(colour + 2 * dz, g)
                peer = sec_peer(dx, dz)
                copies.append((two_vectors(peer[1]) if is_b else None, pltpu.make_async_remote_copy(
                    src_ref=psi_hbm.at[1 if is_b else vector_a(peer[1]), 0, rows, cols],
                    dst_ref=bufs[ch].at[slot, rows, :],
                    send_sem=s1_send.at[ch, g, i], recv_sem=s1_recv.at[ch, g, i],
                    device_id=peer, device_id_type=MESH)))
            first[ch].append(copies)
            rows = shard_rows(colour, g)
            share[ch].append([pltpu.make_async_remote_copy(
                src_ref=bufs[ch].at[1:8, rows, :], dst_ref=bufs[ch].at[1:8, rows, :],
                send_sem=sh_send.at[ch, g, i], recv_sem=sh_recv.at[ch, g, i],
                device_id=(near[i], sec), device_id_type=MESH) for i in range(3)])
            copies = []
            for n, q in enumerate((0, 3, 1, 2)):
                rows = shard_rows(colour + q, g)
                copies.append(pltpu.make_async_remote_copy(
                    src_ref=bufs[ch].at[1:8, rows, :], dst_ref=bufs[ch].at[1:8, rows, :],
                    send_sem=mt_send.at[ch, g, n], recv_sem=mt_recv.at[ch, g, n],
                    device_id=(mate, sec), device_id_type=MESH))
            cross[ch].append(copies)
    loads = [pltpu.make_async_copy(left_hbm, left, load_sem.at[0]),
             pltpu.make_async_copy(right_hbm, right, load_sem.at[1])]

    def when(condition, action):
        if condition is None:
            action()
        else:
            pl.when(condition)(action)

    def start_first(ch):
        for g in range(SPLIT):
            for condition, copy in first[ch][g]:
                when(condition, copy.start)

    def step_share(ch, g):
        for _, copy in first[ch][g]:
            copy.wait_recv()
        for copy in share[ch][g]:
            copy.start()
        cross[ch][g][0].start()

    def step_cross(ch, g):
        for i in range(3):
            share[ch][g][i].wait_recv()
            cross[ch][g][i + 1].start()

    def step_ready(ch):
        for copies in cross[ch]:
            for copy in copies:
                copy.wait_recv()
        own_copies[ch].wait()

    own_copies[0].start()
    own_copies[1].start()
    pl.semaphore_wait(barrier, len(routes) + peers - 1)
    start_first(0)
    for copy in loads:
        copy.start()
    start_first(1)

    def slot_of(k, target):
        source = jnp.int32(0)
        for s in range(sectors):
            source = source + jnp.where(targets[k, s] == target, s, 0)
        d = lax.rem(lax.rem(source, 4) - x + 4, 4)
        same = source // 4 == zh
        return jnp.where(same, jnp.where(d == 0, 0, jnp.where(d == 1, 1, jnp.where(d == 3, 2, 4))),
                         jnp.where(d == 0, 3, jnp.where(d == 1, 5, jnp.where(d == 3, 6, 7))))

    def compute(unit, ch, start=0, stop=None):
        h = ch % HALF
        cols = slice(h * width, (h + 1) * width)
        at = unit

        def body(i, carry):
            mids = []
            for u in range(UNROLL):
                k = i * UNROLL + u
                mids.append(jnp.dot(left[k], bufs[ch][slot_of(k, unit_target[unit])],
                                    preferred_element_type=F32).astype(BF16))
            total = None
            for u in range(UNROLL):
                part = lax.dot_general(mids[u], right[i * UNROLL + u, :, cols], (((1,), (1,)), ((), ())),
                                       preferred_element_type=F32)
                total = part if total is None else total + part
            acc[at] += total.reshape(chips, 2, rows_out, size)
            return carry

        if h == 0 and start == 0:
            acc[at] = jnp.zeros(acc.shape[1:], F32)
        lax.fori_loop(start // UNROLL, (ops if stop is None else stop) // UNROLL, body, 0)

    chip = op // 2

    def pair_copy(unit):
        return pltpu.make_async_remote_copy(
            src_ref=sbuf.at[unit], dst_ref=mbuf.at[unit],
            send_sem=pr_send.at[unit], recv_sem=pr_recv.at[unit],
            device_id=(mate, sec), device_id_type=MESH)

    def reduce_copy(unit, j):
        to = lax.rem(chip + j, chips)
        return pltpu.make_async_remote_copy(
            src_ref=tbuf.at[unit, to],
            dst_ref=rbuf.at[unit_vector[unit], chip],
            send_sem=rs_send.at[unit, j], recv_sem=rs_recv.at[unit_vector[unit], chip],
            device_id=(2 * to + core, unit_target[unit]), device_id_type=MESH)

    def keep_copy(unit):
        return pltpu.make_async_copy(tbuf.at[unit, chip], rbuf.at[unit_vector[unit], chip], self_sem.at[0])

    def send_pair(unit):
        sbuf[unit] = acc[unit, :, 1 - core].astype(BF16)
        pair_copy(unit).start()

    def send(unit):
        pair_copy(unit).wait_recv()
        tbuf[unit] = (acc[unit, :, core] + mbuf[unit].astype(F32)).astype(BF16)
        for j in (4, 5, 3, 6, 2, 7, 1):
            reduce_copy(unit, j).start()
        mine = unit_target[unit] == sec
        pl.when(jnp.logical_not(mine))(lambda: reduce_copy(unit, 0).start())
        pl.when(mine)(lambda: keep_copy(unit).start())

    step_share(0, 0)
    step_share(0, 1)
    step_share(1, 0)
    step_cross(0, 0)
    step_share(1, 1)
    step_cross(0, 1)
    start_first(2)
    start_first(3)

    @pl.when(both)
    def _():
        own_copies[2].start()
        own_copies[3].start()

    for copy in loads:
        copy.wait()
    step_ready(0)
    compute(0, 0)
    for g in range(SPLIT):
        step_cross(1, g)

    @pl.when(both)
    def _():
        for ch in (2, 3):
            for g in range(SPLIT):
                step_share(ch, g)

    compute(1, 0)
    step_ready(1)
    compute(0, 1)
    send_pair(0)

    @pl.when(both)
    def _():
        for g in range(SPLIT):
            step_cross(2, g)

    compute(1, 1, 0, ops // 2)
    send(0)
    compute(1, 1, ops // 2)
    send_pair(1)

    @pl.when(both)
    def _():
        for g in range(SPLIT):
            step_cross(3, g)
        step_ready(2)
        compute(2, 2)
        send(1)
        step_ready(3)
        compute(2, 3)

    @pl.when(jnp.logical_not(both))
    def _():
        compute(2, 0)
        send(1)
        compute(2, 1)

    send_pair(2)
    send(2)

    for unit in range(UNITS):
        pl.when(unit_target[unit] == sec)(lambda: keep_copy(unit).wait())
    for v in range(vectors):
        def arrival(j):
            source = lax.rem(chip + j, chips)
            return pltpu.make_async_remote_copy(
                src_ref=tbuf.at[0, chip], dst_ref=rbuf.at[v, source],
                send_sem=rs_send.at[0, j], recv_sem=rs_recv.at[v, source],
                device_id=(2 * source + core, sec), device_id_type=MESH)

        pl.when((sectors * v + sec) // UNITS != sec)(lambda: arrival(0).wait_recv())
        for j in range(1, chips):
            arrival(j).wait_recv()
        total = rbuf[v, 0].astype(F32)
        for j in range(1, chips):
            total = total + rbuf[v, j].astype(F32)
        out_ref[v, 0] = total.astype(BF16)

    for ch in range(chunks):
        for g in range(SPLIT):
            for condition, copy in first[ch][g]:
                when(condition, copy.wait_send)

        def sent():
            for g in range(SPLIT):
                for copy in share[ch][g] + cross[ch][g]:
                    copy.wait_send()

        when(both if ch >= HALF else None, sent)
    for unit in range(UNITS):
        pair_copy(unit).wait_send()
        for j in range(1, chips):
            reduce_copy(unit, j).wait_send()
        pl.when(unit_target[unit] != sec)(lambda: reduce_copy(unit, 0).wait_send())


def per_device(wavefunction, left_ops, right_ops, targets):
    vectors, _, size, _ = wavefunction.shape
    ops = left_ops.shape[0]
    chunks = 2 * HALF
    width = size // HALF
    dma = pltpu.SemaphoreType.DMA
    scratch = [pltpu.VMEM((8, size, width), BF16) for _ in range(chunks)] + [
        pltpu.VMEM((ops, size, size), BF16),
        pltpu.VMEM((ops, size, size), BF16),
        pltpu.VMEM((UNITS, 8, 2, size // 16, size), F32),
        pltpu.VMEM((UNITS, 8, size // 16, size), BF16),
        pltpu.VMEM((UNITS, 8, size // 16, size), BF16),
        pltpu.VMEM((UNITS, 8, size // 16, size), BF16),
        pltpu.VMEM((vectors, 8, size // 16, size), BF16),
        dma((chunks, SPLIT, 7)), dma((chunks, SPLIT, 7)), dma((chunks, SPLIT, 3)), dma((chunks, SPLIT, 3)),
        dma((chunks, SPLIT, 4)), dma((chunks, SPLIT, 4)),
        dma((UNITS,)), dma((UNITS,)), dma((UNITS, 8)), dma((vectors, 8)), dma((2,)), dma((chunks,)), dma((1,)),
    ]
    hbm = pl.BlockSpec(memory_space=pl.ANY)
    return pl.pallas_call(
        kernel,
        out_shape=jax.ShapeDtypeStruct((vectors, 1, size // 16, size), BF16),
        in_specs=[hbm, hbm, hbm, pl.BlockSpec(memory_space=pltpu.SMEM)],
        out_specs=pl.BlockSpec(memory_space=pltpu.VMEM),
        scratch_shapes=scratch,
        compiler_params=pltpu.CompilerParams(
            collective_id=0, has_side_effects=True, vmem_limit_bytes=62 * 2**20),
        name="sigma",
    )(wavefunction, left_ops, right_ops, targets)


def solution(mesh):
    return jax.shard_map(
        per_device,
        mesh=mesh,
        in_specs=(
            P(None, "sec", None, None),
            P("op", None, None),
            P("op", None, None),
            P("op", None),
        ),
        out_specs=P(None, "sec", "op", None),
        check_vma=False,
    )
```
